32 devices in a mesh: gx: 4 (over y, core), gy: 4 (over z), gz: 2 (over x).
Axes of the slice: x: 2, y: 2, z: 4, core: 2. Of those that a mesh axis runs over, the one named last changes fastest.
Arguments:
- right_side: bfloat16 [16384, 1024], P(('gx', 'gy', 'gz')), may hold values from -6 to 6
- projector: bfloat16 [16384, 256], P(('gx', 'gy', 'gz')), may hold values from -0.25 to 0.25
- translations: bfloat16 [32, 5, 256, 512], P(('gx', 'gy', 'gz')), may hold values from -0.25 to 0.25
- evaluator: bfloat16 [16384, 256], P(('gx', 'gy', 'gz')), may hold values from -0.375 to 0.375
Outputs:
- product: bfloat16 [16384, 1024], P(('gx', 'gy', 'gz'))
The draws below stay inside these ranges and needn't reach their ends.
All inputs are finite; a program needn't handle non-finite values.
Results may differ from the reference program's by a relative error of at most 0.02.
Values may be sent and summed in bfloat16 or wider, within the bound.
A program may use at most 64 MiB of HBM per device.

```python
import jax
import jax.numpy as jnp
from jax import lax

RANK = 256
RHS = 1024
LEAF = 512
BOXES = 32
ROWS = 16384
BITS_GX = 2
BITS_GY = 2
BITS_GZ = 1
LEVELS = 5
N_GY = 4
N_GZ = 2


def block_levels(key, extent, split, least, high):
    loudness = 1.0
    for position, shards_of in split:
        steps = jax.random.uniform(jax.random.fold_in(jax.random.fold_in(key, 6), position), (shards_of,), jnp.float32, least / len(split), high / len(split))
        loudness = loudness * jnp.repeat(jnp.exp(steps), extent[position] // shards_of).reshape((-1,) + (1,) * (len(extent) - 1 - position))
    return loudness


def normal_values(own_key, dims, width, bound, split=(), dtype=jnp.bfloat16):
    factor_of = block_levels(own_key, dims, split, -0.22, 0.18) if split else 1.0
    values = jax.random.normal(own_key, dims, jnp.float32) * width * factor_of
    return jnp.minimum(jnp.maximum(values, -bound), bound).astype(dtype)


def setup_inputs(seed: int = 0) -> dict:
    arg_keys = jax.random.split(jax.random.key(seed), 5)
    right_side = normal_values(arg_keys[0], (ROWS, RHS), 1.0, 6.0, ((0, 32),))
    projector = normal_values(arg_keys[1], (ROWS, RANK), LEAF ** -0.5, 0.25, ((0, 32),))
    translations = normal_values(arg_keys[2], (BOXES, LEVELS, RANK, 2 * RANK), (2 * RANK) ** -0.5, 0.25, ((0, 32),))
    evaluator = normal_values(arg_keys[3], (ROWS, RANK), RANK ** -0.5, 0.375, ((0, 32),))
    return {"right_side": right_side, "projector": projector, "translations": translations, "evaluator": evaluator}


def project_box(bundle):
    return jnp.dot(bundle[0].T, bundle[1], preferred_element_type=jnp.float32).astype(jnp.bfloat16)


def translate_box(bundle):
    mapping, own_part, partner = bundle
    total = jnp.dot(mapping[:, :RANK], own_part, preferred_element_type=jnp.float32)
    total = total + jnp.dot(mapping[:, RANK:], partner, preferred_element_type=jnp.float32)
    return total.astype(jnp.bfloat16)


def evaluate_box(bundle):
    return jnp.dot(bundle[0], bundle[1], preferred_element_type=jnp.float32).astype(jnp.bfloat16)


def reference(right_side, projector, translations, evaluator):
    source_rows = right_side.reshape(BOXES, LEAF, RHS)
    project_rows = projector.reshape(BOXES, LEAF, RANK)
    evaluate_rows = evaluator.reshape(BOXES, LEAF, RANK)
    coefficients = lax.map(project_box, (project_rows, source_rows))
    strides = [N_GY * N_GZ * 2 ** k for k in range(BITS_GX)]
    strides = strides + [N_GZ * 2 ** k for k in range(BITS_GY)]
    strides = strides + [2 ** k for k in range(BITS_GZ)]
    for height, stride in enumerate(strides):
        viewed = coefficients.reshape(BOXES // (2 * stride), 2, stride, RANK, RHS)
        partner = viewed[:, ::-1].reshape(BOXES, RANK, RHS)
        coefficients = lax.map(translate_box, (translations[:, height], coefficients, partner))
    result = lax.map(evaluate_box, (evaluate_rows, coefficients))
    return result.reshape(ROWS, RHS)
```

```python
import functools

import jax
import jax.numpy as jnp
from jax import lax
from jax.experimental import pallas as pl
from jax.experimental.pallas import tpu as pltpu
from jax.sharding import PartitionSpec as P

MESH = pl.DeviceIdType.MESH
PIECE = 128


def level_plan(sizes):
    return [(axis, bit) for axis, size in sizes for bit in range(size.bit_length() - 1)]


def step_order(pieces, levels):
    offset = [0.0, 0.3] + [0.3 + 1.2 * k for k in range(1, levels)]
    steps = [(p + offset[l], -l, p, l) for p in range(pieces) for l in range(levels + 1)]
    return [(p, l) for _, _, p, l in sorted(steps)]


def kernel(plan, steps, right_hbm, projector_hbm, translation_hbm, out_ref,
           right, projector, projector_t, mapping, stack,
           right_sem, projector_sem, mapping_sem, send_sem, recv_sem):
    rank = out_ref.shape[0]
    pieces = out_ref.shape[1] // PIECE
    levels = len(plan)

    def columns(p):
        return pl.ds(p * PIECE, PIECE)

    loads = [pltpu.make_async_copy(projector_hbm, projector, projector_sem)]
    right_loads = [
        pltpu.make_async_copy(right_hbm.at[:, columns(p)], right.at[p], right_sem.at[p])
        for p in range(pieces)
    ]
    mapping_loads = [
        pltpu.make_async_copy(translation_hbm.at[l], mapping.at[l], mapping_sem.at[l])
        for l in range(levels)
    ]
    loads[0].start()
    right_loads[0].start()
    for copy in mapping_loads[:2] + right_loads[1:] + mapping_loads[2:]:
        copy.start()

    partners = []
    for axis, bit in plan:
        me = lax.axis_index(axis)
        step = 1 << bit
        partners.append({axis: me + step - 2 * step * ((me // step) % 2)})
    barrier = pltpu.get_barrier_semaphore()
    for partner in partners:
        pl.semaphore_signal(barrier, inc=1, device_id=partner, device_id_type=MESH)

    def exchange(p, l):
        return pltpu.make_async_remote_copy(
            src_ref=stack.at[l, p, pl.ds(0, rank)],
            dst_ref=stack.at[l, p, pl.ds(rank, rank)],
            send_sem=send_sem.at[l, p],
            recv_sem=recv_sem.at[l, p],
            device_id=partners[l],
            device_id_type=MESH,
        )

    loads[0].wait()
    projector_t[...] = projector[...].T
    first = True
    mapped = set()
    for p, l in steps:
        if l == 0:
            right_loads[p].wait()
            value = jnp.dot(projector_t[...], right[p], preferred_element_type=jnp.float32)
        else:
            if l not in mapped:
                mapping_loads[l - 1].wait()
                mapped.add(l)
            exchange(p, l - 1).wait_recv()
            value = jnp.dot(mapping[l - 1], stack[l - 1, p], preferred_element_type=jnp.float32)
        value = value.astype(jnp.bfloat16)
        if l < levels:
            stack[l, p, pl.ds(0, rank)] = value
            if first:
                pl.semaphore_wait(barrier, levels)
                first = False
            exchange(p, l).start()
        else:
            out_ref[:, columns(p)] = value
    for l in range(levels):
        for p in range(pieces):
            exchange(p, l).wait_send()


def body(sizes, right_side, projector, translations, evaluator):
    plan = level_plan(sizes)
    levels = len(plan)
    leaf, width = right_side.shape
    rank = projector.shape[1]
    pieces = width // PIECE
    half = jnp.bfloat16
    any_space = pl.BlockSpec(memory_space=pl.ANY)
    coefficients = pl.pallas_call(
        functools.partial(kernel, plan, step_order(pieces, levels)),
        out_shape=jax.ShapeDtypeStruct((rank, width), half),
        in_specs=[any_space] * 3,
        out_specs=pl.BlockSpec(memory_space=pltpu.VMEM),
        scratch_shapes=[
            pltpu.VMEM((pieces, leaf, PIECE), half),
            pltpu.VMEM((leaf, rank), half),
            pltpu.VMEM((rank, leaf), half),
            pltpu.VMEM((levels, rank, 2 * rank), half),
            pltpu.VMEM((levels, pieces, 2 * rank, PIECE), half),
            pltpu.SemaphoreType.DMA((pieces,)),
            pltpu.SemaphoreType.DMA,
            pltpu.SemaphoreType.DMA((levels,)),
            pltpu.SemaphoreType.DMA((levels, pieces)),
            pltpu.SemaphoreType.DMA((levels, pieces)),
        ],
        compiler_params=pltpu.CompilerParams(collective_id=0, has_side_effects=True),
    )(right_side, projector, translations[0])
    return jnp.dot(evaluator, coefficients, preferred_element_type=jnp.float32).astype(half)


def solution(mesh):
    placed = (
        P(("gx", "gy", "gz"), None),
        P(("gx", "gy", "gz"), None),
        P(("gx", "gy", "gz"), None, None, None),
        P(("gx", "gy", "gz"), None),
    )
    sizes = [(axis, mesh.shape[axis]) for axis in ("gx", "gy", "gz")]
    return jax.shard_map(
        functools.partial(body, sizes), mesh=mesh, in_specs=placed,
        out_specs=P(("gx", "gy", "gz"), None), check_vma=False,
    )
```

```python
import functools

import jax
import jax.numpy as jnp
from jax import lax
from jax.experimental import pallas as pl
from jax.experimental.pallas import tpu as pltpu
from jax.sharding import PartitionSpec as P

MESH = pl.DeviceIdType.MESH
PIECE = 128


def level_plan(sizes):
    return [(axis, bit) for axis, size in sizes for bit in range(size.bit_length() - 1)]


def step_order(plan, pieces):
    steps = []
    when = 0.0
    for l in range(len(plan) + 1):
        steps += [(p + when, p, l, False) for p in range(pieces)]
        if l < len(plan):
            if relayed(plan[l]):
                when += 1.1
                steps += [(p + when, p, l, True) for p in range(pieces)]
            when += 0.4 if l == 0 else 1.0
    steps.sort(key=lambda step: (step[0], -step[2]))
    return [step[1:] for step in steps]


def relayed(level):
    return level == ("gy", 1)


def kernel(plan, steps, right_hbm, projector_hbm, translation_hbm, out_ref,
           right, projector, projector_t, mapping, stack, relay,
           right_sem, projector_sem, mapping_sem, send_sem, recv_sem,
           relay_send, relay_recv):
    rank = out_ref.shape[0]
    pieces = out_ref.shape[1] // PIECE
    levels = len(plan)
    has_relay = any(relayed(level) for level in plan)

    def columns(p):
        return pl.ds(p * PIECE, PIECE)

    projector_load = pltpu.make_async_copy(projector_hbm, projector, projector_sem)
    right_loads = [
        pltpu.make_async_copy(right_hbm.at[:, columns(p)], right.at[p], right_sem.at[p])
        for p in range(pieces)
    ]
    mapping_loads = [
        pltpu.make_async_copy(translation_hbm.at[l], mapping.at[l], mapping_sem.at[l])
        for l in range(levels)
    ]
    projector_load.start()
    right_loads[0].start()
    for copy in mapping_loads[:2] + right_loads[1:] + mapping_loads[2:]:
        copy.start()

    place = lax.axis_index("gy")
    side = (place // 2) % 2
    towards = place + 1 - 2 * side
    middle = (place % 2 + side) % 2

    partners = []
    for axis, bit in plan:
        me = lax.axis_index(axis)
        step = 1 << bit
        partners.append({axis: me + step - 2 * step * ((me // step) % 2)})
    barrier = pltpu.get_barrier_semaphore()
    direct = [partner for partner, level in zip(partners, plan) if not relayed(level)]
    for partner in direct:
        pl.semaphore_signal(barrier, inc=1, device_id=partner, device_id_type=MESH)
    if has_relay:
        @pl.when(middle == 1)
        def _():
            pl.semaphore_signal(
                barrier, inc=1, device_id={"gy": towards}, device_id_type=MESH
            )

    def exchange(p, l):
        if relayed(plan[l]):
            return pltpu.make_async_remote_copy(
                src_ref=stack.at[l, p, pl.ds(0, rank)],
                dst_ref=relay.at[side, p],
                send_sem=send_sem.at[l, p],
                recv_sem=relay_recv.at[side, p],
                device_id={"gy": towards},
                device_id_type=MESH,
            )
        return pltpu.make_async_remote_copy(
            src_ref=stack.at[l, p, pl.ds(0, rank)],
            dst_ref=stack.at[l, p, pl.ds(rank, rank)],
            send_sem=send_sem.at[l, p],
            recv_sem=recv_sem.at[l, p],
            device_id=partners[l],
            device_id_type=MESH,
        )

    def forward(p, l, down):
        return pltpu.make_async_remote_copy(
            src_ref=relay.at[down, p],
            dst_ref=stack.at[l, p, pl.ds(rank, rank)],
            send_sem=relay_send.at[down, p],
            recv_sem=recv_sem.at[l, p],
            device_id={"gy": place + 1 - 2 * down},
            device_id_type=MESH,
        )

    def arrived(p, down):
        return pltpu.make_async_copy(relay.at[down, p], relay.at[down, p], relay_recv.at[down, p])

    def landed(p, l):
        half = stack.at[l, p, pl.ds(rank, rank)]
        return pltpu.make_async_copy(half, half, recv_sem.at[l, p])

    projector_load.wait()
    projector_t[...] = projector[...].T
    first = True
    mapped = set()
    for p, l, is_relay in steps:
        if is_relay:
            @pl.when(middle == 1)
            def _():
                for down in range(2):
                    arrived(p, down).wait()
                    forward(p, l, down).start()
            continue
        if l == 0:
            right_loads[p].wait()
            value = jnp.dot(projector_t[...], right[p], preferred_element_type=jnp.float32)
        else:
            if l not in mapped:
                mapping_loads[l - 1].wait()
                mapped.add(l)
            landed(p, l - 1).wait()
            value = jnp.dot(mapping[l - 1], stack[l - 1, p], preferred_element_type=jnp.float32)
        value = value.astype(jnp.bfloat16)
        if l < levels:
            stack[l, p, pl.ds(0, rank)] = value
            if first:
                pl.semaphore_wait(barrier, len(direct) + (middle if has_relay else 0))
                first = False
            exchange(p, l).start()
        else:
            out_ref[:, columns(p)] = value
    for l in range(levels):
        for p in range(pieces):
            exchange(p, l).wait_send()
    if has_relay:
        @pl.when(middle == 1)
        def _():
            for l in range(levels):
                if relayed(plan[l]):
                    for p in range(pieces):
                        for down in range(2):
                            forward(p, l, down).wait_send()


def evaluate_kernel(evaluator, coefficients, out):
    out[...] = jnp.dot(
        evaluator[...], coefficients[...], preferred_element_type=jnp.float32
    ).astype(out.dtype)


def body(sizes, right_side, projector, translations, evaluator):
    plan = level_plan(sizes)
    levels = len(plan)
    leaf, width = right_side.shape
    rank = projector.shape[1]
    pieces = width // PIECE
    half = jnp.bfloat16
    any_space = pl.BlockSpec(memory_space=pl.ANY)
    coefficients = pl.pallas_call(
        functools.partial(kernel, plan, step_order(plan, pieces)),
        out_shape=jax.ShapeDtypeStruct((rank, width), half),
        in_specs=[any_space] * 3,
        out_specs=pl.BlockSpec(memory_space=pltpu.VMEM),
        scratch_shapes=[
            pltpu.VMEM((pieces, leaf, PIECE), half),
            pltpu.VMEM((leaf, rank), half),
            pltpu.VMEM((rank, leaf), half),
            pltpu.VMEM((levels, rank, 2 * rank), half),
            pltpu.VMEM((levels, pieces, 2 * rank, PIECE), half),
            pltpu.VMEM((2, pieces, rank, PIECE), half),
            pltpu.SemaphoreType.DMA((pieces,)),
            pltpu.SemaphoreType.DMA,
            pltpu.SemaphoreType.DMA((levels,)),
            pltpu.SemaphoreType.DMA((levels, pieces)),
            pltpu.SemaphoreType.DMA((levels, pieces)),
            pltpu.SemaphoreType.DMA((2, pieces)),
            pltpu.SemaphoreType.DMA((2, pieces)),
        ],
        compiler_params=pltpu.CompilerParams(collective_id=0, has_side_effects=True),
    )(right_side, projector, translations[0])
    rows = leaf // 4
    return pl.pallas_call(
        evaluate_kernel,
        out_shape=jax.ShapeDtypeStruct((leaf, width), half),
        grid=(4,),
        in_specs=[
            pl.BlockSpec((rows, rank), lambda i: (i, 0)),
            pl.BlockSpec((rank, width), lambda i: (0, 0)),
        ],
        out_specs=pl.BlockSpec((rows, width), lambda i: (i, 0)),
    )(evaluator, coefficients)


def solution(mesh):
    placed = (
        P(("gx", "gy", "gz"), None),
        P(("gx", "gy", "gz"), None),
        P(("gx", "gy", "gz"), None, None, None),
        P(("gx", "gy", "gz"), None),
    )
    sizes = [(axis, mesh.shape[axis]) for axis in ("gx", "gy", "gz")]
    return jax.shard_map(
        functools.partial(body, sizes), mesh=mesh, in_specs=placed,
        out_specs=P(("gx", "gy", "gz"), None), check_vma=False,
    )
```

```python
import functools

import jax
import jax.numpy as jnp
from jax import lax
from jax.experimental import pallas as pl
from jax.experimental.pallas import tpu as pltpu
from jax.sharding import PartitionSpec as P

MESH = pl.DeviceIdType.MESH
PIECE = 128


def level_plan(sizes):
    return [(axis, bit) for axis, size in sizes for bit in range(size.bit_length() - 1)]


def step_order(pieces, levels):
    offset = [0.0, 0.3] + [0.3 + 1.2 * k for k in range(1, levels)]
    steps = [(0.6 * p + offset[l], -l, p, l) for p in range(pieces) for l in range(levels + 1)]
    return [(p, l) for _, _, p, l in sorted(steps)]


def kernel(plan, steps, right_hbm, projector_hbm, translation_hbm, evaluator_hbm, out_hbm,
           right, projector, projector_t, mapping, stack, evaluator, out,
           right_sem, projector_sem, mapping_sem, send_sem, recv_sem,
           evaluator_sem, out_sem):
    rank = projector.shape[1]
    pieces = right.shape[0]
    levels = len(plan)

    def columns(p):
        return pl.ds(p * PIECE, PIECE)

    loads = [pltpu.make_async_copy(projector_hbm, projector, projector_sem)]
    right_loads = [
        pltpu.make_async_copy(right_hbm.at[:, columns(p)], right.at[p], right_sem.at[p])
        for p in range(pieces)
    ]
    mapping_loads = [
        pltpu.make_async_copy(translation_hbm.at[l], mapping.at[l], mapping_sem.at[l])
        for l in range(levels)
    ]
    evaluator_load = pltpu.make_async_copy(evaluator_hbm, evaluator, evaluator_sem)
    loads[0].start()
    right_loads[0].start()
    for copy in mapping_loads[:2] + right_loads[1:] + mapping_loads[2:] + [evaluator_load]:
        copy.start()

    partners = []
    for axis, bit in plan:
        me = lax.axis_index(axis)
        step = 1 << bit
        partners.append({axis: me + step - 2 * step * ((me // step) % 2)})
    barrier = pltpu.get_barrier_semaphore()
    for partner in partners:
        pl.semaphore_signal(barrier, inc=1, device_id=partner, device_id_type=MESH)

    def store(p):
        return pltpu.make_async_copy(out.at[p], out_hbm.at[:, columns(p)], out_sem.at[p])

    def exchange(p, l):
        return pltpu.make_async_remote_copy(
            src_ref=stack.at[l, p, pl.ds(0, rank)],
            dst_ref=stack.at[l, p, pl.ds(rank, rank)],
            send_sem=send_sem.at[l, p],
            recv_sem=recv_sem.at[l, p],
            device_id=partners[l],
            device_id_type=MESH,
        )

    loads[0].wait()
    projector_t[...] = projector[...].T
    first = True
    mapped = set()
    for p, l in steps:
        if l == 0:
            right_loads[p].wait()
            value = jnp.dot(projector_t[...], right[p], preferred_element_type=jnp.float32)
        else:
            if l not in mapped:
                mapping_loads[l - 1].wait()
                mapped.add(l)
            exchange(p, l - 1).wait_recv()
            value = jnp.dot(mapping[l - 1], stack[l - 1, p], preferred_element_type=jnp.float32)
        value = value.astype(jnp.bfloat16)
        if l < levels:
            stack[l, p, pl.ds(0, rank)] = value
            if first:
                pl.semaphore_wait(barrier, levels)
                first = False
            exchange(p, l).start()
        else:
            if p == 0:
                evaluator_load.wait()
            product = jnp.dot(evaluator[...], value, preferred_element_type=jnp.float32)
            out[p] = product.astype(jnp.bfloat16)
            store(p).start()
    for l in range(levels):
        for p in range(pieces):
            exchange(p, l).wait_send()
    for p in range(pieces):
        store(p).wait()


def body(sizes, right_side, projector, translations, evaluator):
    plan = level_plan(sizes)
    levels = len(plan)
    leaf, width = right_side.shape
    rank = projector.shape[1]
    pieces = width // PIECE
    half = jnp.bfloat16
    any_space = pl.BlockSpec(memory_space=pl.ANY)
    return pl.pallas_call(
        functools.partial(kernel, plan, step_order(pieces, levels)),
        out_shape=jax.ShapeDtypeStruct((leaf, width), half),
        in_specs=[any_space] * 4,
        out_specs=any_space,
        scratch_shapes=[
            pltpu.VMEM((pieces, leaf, PIECE), half),
            pltpu.VMEM((leaf, rank), half),
            pltpu.VMEM((rank, leaf), half),
            pltpu.VMEM((levels, rank, 2 * rank), half),
            pltpu.VMEM((levels, pieces, 2 * rank, PIECE), half),
            pltpu.VMEM((leaf, rank), half),
            pltpu.VMEM((pieces, leaf, PIECE), half),
            pltpu.SemaphoreType.DMA((pieces,)),
            pltpu.SemaphoreType.DMA,
            pltpu.SemaphoreType.DMA((levels,)),
            pltpu.SemaphoreType.DMA((levels, pieces)),
            pltpu.SemaphoreType.DMA((levels, pieces)),
            pltpu.SemaphoreType.DMA,
            pltpu.SemaphoreType.DMA((pieces,)),
        ],
        compiler_params=pltpu.CompilerParams(collective_id=0, has_side_effects=True),
    )(right_side, projector, translations[0], evaluator)


def solution(mesh):
    placed = (
        P(("gx", "gy", "gz"), None),
        P(("gx", "gy", "gz"), None),
        P(("gx", "gy", "gz"), None, None, None),
        P(("gx", "gy", "gz"), None),
    )
    sizes = [(axis, mesh.shape[axis]) for axis in ("gx", "gy", "gz")]
    return jax.shard_map(
        functools.partial(body, sizes), mesh=mesh, in_specs=placed,
        out_specs=P(("gx", "gy", "gz"), None), check_vma=False,
    )
```

```python
import functools

import jax
import jax.numpy as jnp
from jax import lax
from jax.experimental import pallas as pl
from jax.experimental.pallas import tpu as pltpu
from jax.sharding import PartitionSpec as P

MESH = pl.DeviceIdType.MESH
PIECE = 128


def level_plan(sizes):
    return [(axis, bit) for axis, size in sizes for bit in range(size.bit_length() - 1)]


def step_order(pieces, levels):
    offset = [0.0, 0.3] + [0.3 + 1.2 * k for k in range(1, levels)]
    steps = [(0.6 * p + offset[l], -l, p, l) for p in range(pieces) for l in range(levels + 1)]
    return [(p, l) for _, _, p, l in sorted(steps)]


def kernel(plan, steps, right_hbm, projector_hbm, translation_hbm, evaluator_hbm, out_hbm,
           right, projector, projector_t, mapping, stack, evaluator, out,
           right_sem, projector_sem, mapping_sem, send_sem, recv_sem,
           evaluator_sem, out_sem):
    rank = projector.shape[1]
    pieces = right.shape[0]
    levels = len(plan)

    def columns(p):
        return pl.ds(p * PIECE, PIECE)

    loads = [pltpu.make_async_copy(projector_hbm, projector, projector_sem)]
    right_loads = [
        pltpu.make_async_copy(right_hbm.at[:, columns(p)], right.at[p], right_sem.at[p])
        for p in range(pieces)
    ]
    mapping_loads = [
        pltpu.make_async_copy(translation_hbm.at[l], mapping.at[l], mapping_sem.at[l])
        for l in range(levels)
    ]
    evaluator_load = pltpu.make_async_copy(evaluator_hbm, evaluator, evaluator_sem)
    loads[0].start()
    right_loads[0].start()

    partners = []
    for axis, bit in plan:
        me = lax.axis_index(axis)
        step = 1 << bit
        partners.append({axis: me + step - 2 * step * ((me // step) % 2)})
    barrier = pltpu.get_barrier_semaphore()
    for partner in partners:
        pl.semaphore_signal(barrier, inc=1, device_id=partner, device_id_type=MESH)

    def store(p):
        return pltpu.make_async_copy(out.at[p], out_hbm.at[:, columns(p)], out_sem.at[p])

    def exchange(p, l):
        return pltpu.make_async_remote_copy(
            src_ref=stack.at[l, p, pl.ds(0, rank)],
            dst_ref=stack.at[l, p, pl.ds(rank, rank)],
            send_sem=send_sem.at[l, p],
            recv_sem=recv_sem.at[l, p],
            device_id=partners[l],
            device_id_type=MESH,
        )

    loads[0].wait()
    right_loads[0].wait()
    for copy in mapping_loads[:2] + right_loads[1:] + mapping_loads[2:] + [evaluator_load]:
        copy.start()
    projector_t[...] = projector[...].T
    first = True
    mapped = set()
    for p, l in steps:
        if l == 0:
            if p > 0:
                right_loads[p].wait()
            value = jnp.dot(projector_t[...], right[p], preferred_element_type=jnp.float32)
        else:
            if l not in mapped:
                mapping_loads[l - 1].wait()
                mapped.add(l)
            exchange(p, l - 1).wait_recv()
            value = jnp.dot(mapping[l - 1], stack[l - 1, p], preferred_element_type=jnp.float32)
        value = value.astype(jnp.bfloat16)
        if l < levels:
            stack[l, p, pl.ds(0, rank)] = value
            if first:
                pl.semaphore_wait(barrier, levels)
                first = False
            exchange(p, l).start()
        else:
            if p == 0:
                evaluator_load.wait()
            product = jnp.dot(evaluator[...], value, preferred_element_type=jnp.float32)
            out[p] = product.astype(jnp.bfloat16)
            store(p).start()
    for l in range(levels):
        for p in range(pieces):
            exchange(p, l).wait_send()
    for p in range(pieces):
        store(p).wait()


def body(sizes, right_side, projector, translations, evaluator):
    plan = level_plan(sizes)
    levels = len(plan)
    leaf, width = right_side.shape
    rank = projector.shape[1]
    pieces = width // PIECE
    half = jnp.bfloat16
    any_space = pl.BlockSpec(memory_space=pl.ANY)
    return pl.pallas_call(
        functools.partial(kernel, plan, step_order(pieces, levels)),
        out_shape=jax.ShapeDtypeStruct((leaf, width), half),
        in_specs=[any_space] * 4,
        out_specs=any_space,
        scratch_shapes=[
            pltpu.VMEM((pieces, leaf, PIECE), half),
            pltpu.VMEM((leaf, rank), half),
            pltpu.VMEM((rank, leaf), half),
            pltpu.VMEM((levels, rank, 2 * rank), half),
            pltpu.VMEM((levels, pieces, 2 * rank, PIECE), half),
            pltpu.VMEM((leaf, rank), half),
            pltpu.VMEM((pieces, leaf, PIECE), half),
            pltpu.SemaphoreType.DMA((pieces,)),
            pltpu.SemaphoreType.DMA,
            pltpu.SemaphoreType.DMA((levels,)),
            pltpu.SemaphoreType.DMA((levels, pieces)),
            pltpu.SemaphoreType.DMA((levels, pieces)),
            pltpu.SemaphoreType.DMA,
            pltpu.SemaphoreType.DMA((pieces,)),
        ],
        compiler_params=pltpu.CompilerParams(collective_id=0, has_side_effects=True),
    )(right_side, projector, translations[0], evaluator)


def solution(mesh):
    placed = (
        P(("gx", "gy", "gz"), None),
        P(("gx", "gy", "gz"), None),
        P(("gx", "gy", "gz"), None, None, None),
        P(("gx", "gy", "gz"), None),
    )
    sizes = [(axis, mesh.shape[axis]) for axis in ("gx", "gy", "gz")]
    return jax.shard_map(
        functools.partial(body, sizes), mesh=mesh, in_specs=placed,
        out_specs=P(("gx", "gy", "gz"), None), check_vma=False,
    )
```

```python
import functools

import jax
import jax.numpy as jnp
from jax import lax
from jax.experimental import pallas as pl
from jax.experimental.pallas import tpu as pltpu
from jax.sharding import PartitionSpec as P

MESH = pl.DeviceIdType.MESH
PIECE = 128


def level_plan(sizes):
    return [(axis, bit) for axis, size in sizes for bit in range(size.bit_length() - 1)]


def step_order(pieces, levels):
    offset = [0.0, 0.3] + [0.3 + 1.2 * k for k in range(1, levels)]
    steps = [(0.6 * p + offset[l], -l, p, l) for p in range(pieces) for l in range(levels + 1)]
    return [(p, l) for _, _, p, l in sorted(steps)]


def kernel(plan, steps, right_hbm, projector_hbm, translation_hbm, evaluator_hbm, out_hbm,
           right, projector, projector_t, mapping, stack, evaluator, out,
           right_sem, projector_sem, mapping_sem, send_sem, recv_sem,
           evaluator_sem, out_sem):
    rank = projector.shape[1]
    pieces = right.shape[0]
    levels = len(plan)

    def columns(p):
        return pl.ds(p * PIECE, PIECE)

    loads = [pltpu.make_async_copy(projector_hbm, projector, projector_sem)]
    right_loads = [
        pltpu.make_async_copy(right_hbm.at[:, columns(p)], right.at[p], right_sem.at[p])
        for p in range(pieces)
    ]
    mapping_loads = [
        pltpu.make_async_copy(translation_hbm.at[l], mapping.at[l], mapping_sem.at[l])
        for l in range(levels)
    ]
    evaluator_load = pltpu.make_async_copy(evaluator_hbm, evaluator, evaluator_sem)
    loads[0].start()
    right_loads[0].start()

    partners = []
    for axis, bit in plan:
        me = lax.axis_index(axis)
        step = 1 << bit
        partners.append({axis: me + step - 2 * step * ((me // step) % 2)})
    barrier = pltpu.get_barrier_semaphore()
    for partner in partners:
        pl.semaphore_signal(barrier, inc=1, device_id=partner, device_id_type=MESH)

    def store(p):
        return pltpu.make_async_copy(out.at[p], out_hbm.at[:, columns(p)], out_sem.at[p])

    def exchange(p, l):
        return pltpu.make_async_remote_copy(
            src_ref=stack.at[l, p, pl.ds(0, rank)],
            dst_ref=stack.at[l, p, pl.ds(rank, rank)],
            send_sem=send_sem.at[l, p],
            recv_sem=recv_sem.at[l, p],
            device_id=partners[l],
            device_id_type=MESH,
        )

    loads[0].wait()
    right_loads[0].wait()
    for copy in mapping_loads[:2] + right_loads[1:] + mapping_loads[2:] + [evaluator_load]:
        copy.start()
    first = True
    mapped = set()
    for p, l in steps:
        if l == 0:
            if p > 0:
                right_loads[p].wait()
            value = lax.dot_general(projector[...], right[p], (((0,), (0,)), ((), ())), preferred_element_type=jnp.float32)
        else:
            if l not in mapped:
                mapping_loads[l - 1].wait()
                mapped.add(l)
            exchange(p, l - 1).wait_recv()
            value = jnp.dot(mapping[l - 1], stack[l - 1, p], preferred_element_type=jnp.float32)
        value = value.astype(jnp.bfloat16)
        if l < levels:
            stack[l, p, pl.ds(0, rank)] = value
            if first:
                pl.semaphore_wait(barrier, levels)
                first = False
            exchange(p, l).start()
        else:
            if p == 0:
                evaluator_load.wait()
            product = jnp.dot(evaluator[...], value, preferred_element_type=jnp.float32)
            out[p] = product.astype(jnp.bfloat16)
            store(p).start()
    for l in range(levels):
        for p in range(pieces):
            exchange(p, l).wait_send()
    for p in range(pieces):
        store(p).wait()


def body(sizes, right_side, projector, translations, evaluator):
    plan = level_plan(sizes)
    levels = len(plan)
    leaf, width = right_side.shape
    rank = projector.shape[1]
    pieces = width // PIECE
    half = jnp.bfloat16
    any_space = pl.BlockSpec(memory_space=pl.ANY)
    return pl.pallas_call(
        functools.partial(kernel, plan, step_order(pieces, levels)),
        out_shape=jax.ShapeDtypeStruct((leaf, width), half),
        in_specs=[any_space] * 4,
        out_specs=any_space,
        scratch_shapes=[
            pltpu.VMEM((pieces, leaf, PIECE), half),
            pltpu.VMEM((leaf, rank), half),
            pltpu.VMEM((rank, leaf), half),
            pltpu.VMEM((levels, rank, 2 * rank), half),
            pltpu.VMEM((levels, pieces, 2 * rank, PIECE), half),
            pltpu.VMEM((leaf, rank), half),
            pltpu.VMEM((pieces, leaf, PIECE), half),
            pltpu.SemaphoreType.DMA((pieces,)),
            pltpu.SemaphoreType.DMA,
            pltpu.SemaphoreType.DMA((levels,)),
            pltpu.SemaphoreType.DMA((levels, pieces)),
            pltpu.SemaphoreType.DMA((levels, pieces)),
            pltpu.SemaphoreType.DMA,
            pltpu.SemaphoreType.DMA((pieces,)),
        ],
        compiler_params=pltpu.CompilerParams(collective_id=0, has_side_effects=True),
    )(right_side, projector, translations[0], evaluator)


def solution(mesh):
    placed = (
        P(("gx", "gy", "gz"), None),
        P(("gx", "gy", "gz"), None),
        P(("gx", "gy", "gz"), None, None, None),
        P(("gx", "gy", "gz"), None),
    )
    sizes = [(axis, mesh.shape[axis]) for axis in ("gx", "gy", "gz")]
    return jax.shard_map(
        functools.partial(body, sizes), mesh=mesh, in_specs=placed,
        out_specs=P(("gx", "gy", "gz"), None), check_vma=False,
    )
```
